32 devices in a mesh: groups: 2 (over y), ctx: 4 (over z), head: 2 (over x), sub: 2 (over core).
Axes of the slice: x: 2, y: 2, z: 4, core: 2. Of those that a mesh axis runs over, the one named last changes fastest.
Arguments:
- queries: bfloat16 [4096, 40, 128], P(('groups', 'ctx', 'sub'), 'head'), parts along dimension 0, may hold values from -35 to 35
- key_rows: bfloat16 [4096, 40, 128], P(('groups', 'ctx', 'sub'), 'head'), parts along dimension 0, may hold values from -4.5 to 4.5
- value_rows: bfloat16 [4096, 40, 128], P(('groups', 'ctx', 'sub'), 'head'), parts along dimension 0, may hold values from -16 to 16
- critical: int32 [64, 40, 16], P(('groups', 'ctx', 'sub'), 'head'), parts along dimension 0, may hold values from 0 to 31, as said below
- branch_weight: bfloat16 [128, 128], replicated, may hold values from -0.5 to 0.5
Outputs:
- attended: bfloat16 [4096, 40, 128], P(('groups', 'ctx', 'sub'), 'head'), parts along dimension 0
The draws below stay inside these ranges and needn't reach their ends.
There are 2 independent parts, one for each index of `groups`. The reference program is written for one: setup_inputs(seed, part) draws one part's arguments, and reference() takes and returns one part's arrays. A program takes and returns all parts, laid end to end along the dimension named above; an argument that names none is the same for every part. Nothing has to cross between parts.
Inputs may be any that keep to these rules, and one draw needn't show every extreme that they name: Each list critical[b, h, :] names 16 different key blocks. Its first entry is b itself, the next 3 are the following blocks of b's segment of 256 consecutive tokens, cyclically within the segment; the other 12 lie in other segments. Over all lists of one segment's query blocks and one group of 20 consecutive heads, at most 58 different (block, head) pairs lie in any one other segment, and exactly 58 in some.
All inputs are finite; a program needn't handle non-finite values.
Results may differ from the reference program's by a relative error of at most 0.004.
Values may be sent and summed in bfloat16 or wider, within the bound.
No kernel may reach another device: no remote copies, remote signals or barrier semaphores. Data moves between devices by JAX's collectives and lax.ppermute only.
A program may use at most 128 MiB of HBM per device.

```python
import jax
import jax.numpy as jnp
from jax import lax

ATTENTION_HEADS = 40
HD = 128
ROWS = 256
TOPK = 16
LOCAL = 4
POOL = 20
SHARDS = 8
H_DEV = 20
LATENT_TOKENS = 2048


def key_table(key):
    first = jax.random.fold_in(jax.random.fold_in(key, 101), 0)
    table = jnp.clip(jax.random.normal(first, (LATENT_TOKENS, ATTENTION_HEADS, HD), jnp.float32), -4.5, 4.5)
    return table


def key_drift(key):
    slope_key = jax.random.fold_in(key, 404)
    slopes = 0.8 + 0.3 * jnp.clip(jax.random.normal(slope_key, (ATTENTION_HEADS, HD), jnp.float32), -2.5, 2.5)
    progress = -1.5 + 3.0 * jnp.arange(LATENT_TOKENS).astype(jnp.float32) / (LATENT_TOKENS - 1)
    return progress[:, None, None] * slopes[None, :, :]


def draw_key_rows(key, part):
    drifted = jnp.clip(key_table(key) + key_drift(key), -4.5, 4.5)
    return drifted.astype(jnp.bfloat16)


def draw_queries(key, part):
    noise_key = jax.random.fold_in(key, 202)
    base = jnp.clip(jax.random.normal(noise_key, (LATENT_TOKENS, ATTENTION_HEADS, HD), jnp.float32), -4.5, 4.5)
    return base.astype(jnp.bfloat16)


def draw_value_rows(key, part):
    first, second, third_fraction = jax.random.split(jax.random.fold_in(key, 303), 3)
    random_noise = jnp.clip(jax.random.normal(first, (LATENT_TOKENS, ATTENTION_HEADS, HD), jnp.float32), -4.5, 4.5)
    channel_index = 0.6 * jnp.clip(jax.random.normal(second, (ATTENTION_HEADS, HD), jnp.float32), -2.5, 2.5)
    linear_ramp = 1.0 + 2.0 * jnp.arange(LATENT_TOKENS).astype(jnp.float32) / (LATENT_TOKENS - 1)
    spike_pattern = jnp.exp(jax.random.uniform(third_fraction, (LATENT_TOKENS // 64, ATTENTION_HEADS), jnp.float32, jnp.log(0.4), jnp.log(2.5)))
    spike_row_list = jnp.repeat(spike_pattern, 64, axis=0)
    output_values = random_noise + channel_index[None, :, :] * (linear_ramp[:, None] * spike_row_list)[:, :, None]
    return output_values.astype(jnp.bfloat16)


def draw_critical(key, part):
    key_perm, key_rot, key_pick = jax.random.split(key, 3)
    group_count = ATTENTION_HEADS // H_DEV
    block_count = ROWS // 64
    other_count = SHARDS - 1
    perms = jax.vmap(lambda one_key: jax.random.permutation(one_key, other_count))(jax.random.split(key_perm, SHARDS * group_count))
    perms = perms.reshape(SHARDS, group_count, other_count)
    rotate = jax.random.randint(key_rot, (SHARDS, group_count), 0, block_count)
    order = jnp.arange(H_DEV * POOL)
    offset = 1 + perms[:, :, order % other_count]
    owner_shard = (jnp.arange(SHARDS)[:, None, None] + offset) % SHARDS
    same_owner = owner_shard[:, :, :, None] == owner_shard[:, :, None, :]
    earlier = order[None, :] < order[:, None]
    rank = jnp.sum(jnp.logical_and(same_owner, earlier[None, None]).astype(jnp.int32), axis=-1)
    block_local = (rank + rotate[:, :, None]) % block_count
    pool_ids = (owner_shard * block_count + block_local).reshape(SHARDS, ATTENTION_HEADS, POOL)
    picks = jax.vmap(lambda one_key: jax.random.permutation(one_key, POOL))(jax.random.split(key_pick, SHARDS * ATTENTION_HEADS))
    picks = picks.reshape(SHARDS, ATTENTION_HEADS, POOL)
    kept = (jnp.arange(block_count)[:, None] * 8 + 8 + jnp.arange(TOPK - LOCAL)[None, :]) % POOL
    chosen = picks[:, :, kept].reshape(SHARDS, ATTENTION_HEADS, block_count * (TOPK - LOCAL))
    remote = jnp.take_along_axis(pool_ids, chosen, axis=2).reshape(SHARDS, ATTENTION_HEADS, block_count, TOPK - LOCAL)
    remote = remote.transpose(0, 2, 1, 3)
    nearby = (jnp.arange(block_count)[:, None] + jnp.arange(LOCAL)[None, :]) % block_count
    nearby = jnp.arange(SHARDS)[:, None, None] * block_count + nearby[None, :, :]
    nearby = jnp.broadcast_to(nearby[:, :, None, :], (SHARDS, block_count, ATTENTION_HEADS, LOCAL))
    lists = jnp.concatenate([nearby, remote], axis=-1).reshape(SHARDS * block_count, ATTENTION_HEADS, TOPK)
    return lists.astype(jnp.int32)


def centred(rng, shape, deviation, most, dtype=jnp.bfloat16):
    result = deviation * jax.random.normal(rng, shape, jnp.float32)
    return jnp.clip(result, min=-most, max=most).astype(dtype)


def setup_inputs(seed: int = 0, part: int = 0) -> dict:
    splits = jax.random.split(jax.random.key(seed), 6)
    part_splits = jax.random.split(jax.random.fold_in(splits[5], part), 6)
    return {
        "queries": draw_queries(jax.random.fold_in(jax.random.fold_in(splits[5], part), 71), part),
        "key_rows": draw_key_rows(jax.random.fold_in(jax.random.fold_in(splits[5], part), 71), part),
        "value_rows": draw_value_rows(jax.random.fold_in(jax.random.fold_in(splits[5], part), 71), part),
        "critical": draw_critical(jax.random.fold_in(jax.random.fold_in(splits[5], part), 71), part),
        "branch_weight": centred(splits[4], (HD, HD), HD ** -0.5, 0.5),
    }


def feature(values_in):
    return jax.nn.elu(values_in) + 1.0


def reference(queries, key_rows, value_rows, critical, branch_weight):
    seq_count, head_count, head_width = queries.shape
    block_count = seq_count // 64
    softmax_scale = head_width ** -0.5
    key_feature = feature(key_rows.astype(jnp.float32)).astype(jnp.bfloat16)
    query_feature = feature(queries.astype(jnp.float32)).astype(jnp.bfloat16)
    kv_state = jnp.einsum("thd,the->hde", key_feature.astype(jnp.float32), value_rows.astype(jnp.float32), precision=lax.Precision.HIGHEST)
    key_total = jnp.sum(key_feature.astype(jnp.float32), axis=0)

    def one_head(inputs):
        query_head, qfeat_head, key_head, value_head, kfeat_head, list_head, head_state_matrix, head_key_total = inputs
        nearby_key_rows = key_head.reshape(block_count, 64, head_width)[list_head].reshape(block_count, -1, head_width)
        nearby_value_rows = value_head.reshape(block_count, 64, head_width)[list_head].reshape(block_count, -1, head_width)
        nearby_key_features = kfeat_head.reshape(block_count, 64, head_width)[list_head].reshape(block_count, -1, head_width)
        query_block_rows = query_head.reshape(block_count, 64, head_width).astype(jnp.float32)
        query_feature_block = qfeat_head.reshape(block_count, 64, head_width).astype(jnp.float32)
        score_matrix = jnp.einsum("twa,tpa->twp", query_block_rows, nearby_key_rows.astype(jnp.float32)) * softmax_scale
        top_score = jnp.max(score_matrix, axis=-1, keepdims=True)
        expo_scores = jnp.exp(score_matrix - top_score)
        softmax_weights = (expo_scores / jnp.sum(expo_scores, axis=-1, keepdims=True)).astype(jnp.bfloat16)
        sparse_output = jnp.einsum("mgw,mwa->mga", softmax_weights.astype(jnp.float32), nearby_value_rows.astype(jnp.float32))
        nearby_score_matrix = jnp.einsum("twa,tpa->twp", query_feature_block, nearby_key_features.astype(jnp.float32))
        nearby_weight_matrix = nearby_score_matrix.astype(jnp.bfloat16)
        nearby_numerator = jnp.einsum("mgw,mwa->mga", nearby_weight_matrix.astype(jnp.float32), nearby_value_rows.astype(jnp.float32))
        nearby_denominator = jnp.sum(nearby_score_matrix, axis=-1)
        linear_numerator = jnp.einsum("gfh,ht->gft", query_feature_block, head_state_matrix, precision=lax.Precision.HIGHEST) - nearby_numerator
        linear_denominator = jnp.einsum("tay,y->ta", query_feature_block, head_key_total, precision=lax.Precision.HIGHEST) - nearby_denominator
        linear_part = (linear_numerator / linear_denominator[..., None]).astype(jnp.bfloat16)
        projected = jnp.dot(linear_part.reshape(-1, head_width), branch_weight, preferred_element_type=jnp.float32)
        mixed_rows = sparse_output.reshape(-1, head_width) + projected
        return mixed_rows.astype(jnp.bfloat16)

    attended = lax.map(one_head, (queries.transpose(1, 0, 2), query_feature.transpose(1, 0, 2), key_rows.transpose(1, 0, 2), value_rows.transpose(1, 0, 2), key_feature.transpose(1, 0, 2), critical.transpose(1, 0, 2), kv_state, key_total))
    return attended.transpose(1, 0, 2)
```

```python
import functools

import jax
import jax.numpy as jnp
from jax import lax
from jax.experimental import pallas as pl
from jax.experimental.pallas import tpu as pltpu
from jax.sharding import PartitionSpec as P

BLOCK = 64


def kernel_feature(values_in):
    wide = values_in.astype(jnp.float32)
    return jnp.where(wide > 0, wide + 1.0, jnp.exp(jnp.minimum(wide, 0.0))).astype(jnp.bfloat16)


def attend_kernel(softmax_scale, parts, lists, *refs):
    query_refs = refs[:parts]
    column_refs = refs[parts : parts + 2]
    weight_ref = refs[parts + 2]
    out_refs = refs[parts + 3 : 2 * parts + 3]
    keys, features, values, totals = refs[2 * parts + 3 :]
    head = pl.program_id(0)
    rows, width = query_refs[0].shape[-2:]
    blocks = rows // BLOCK
    state = jnp.zeros((width, width), jnp.float32)
    for column, ref in enumerate(column_refs):
        for part in range(parts):
            first = (column * parts + part) * blocks
            key = ref[part, 0, 0]
            value = ref[part, 0, 1]
            key_feature = kernel_feature(key)
            keys[first : first + blocks] = key.reshape(blocks, BLOCK, width)
            values[first : first + blocks] = value.reshape(blocks, BLOCK, width)
            features[first : first + blocks] = key_feature.reshape(blocks, BLOCK, width)
            totals[pl.ds(first, blocks), :] = jnp.sum(
                key_feature.astype(jnp.float32).reshape(blocks, BLOCK, width), axis=1
            )
            state = state + lax.dot_general(
                key_feature, value, (((0,), (0,)), ((), ())), preferred_element_type=jnp.float32
            )
    total = jnp.sum(totals[...], axis=0, keepdims=True)
    high = state.astype(jnp.bfloat16)
    left = state - high.astype(jnp.float32)
    middle = left.astype(jnp.bfloat16)
    low = (left - middle.astype(jnp.float32)).astype(jnp.bfloat16)
    by_row = (((1,), (1,)), ((), ()))
    for part in range(parts):
        for block in range(blocks):
            span = slice(block * BLOCK, (block + 1) * BLOCK)
            query = query_refs[part][0, 0, span, :]
            query_feature = kernel_feature(query)
            near = [lists[head, part * blocks + block, j] for j in range(lists.shape[2])]
            near_keys = jnp.concatenate([keys[i] for i in near], axis=0)
            near_features = jnp.concatenate([features[i] for i in near], axis=0)
            near_values = jnp.concatenate([values[i] for i in near], axis=0)
            scores = lax.dot_general(
                query, near_keys, by_row, preferred_element_type=jnp.float32
            )
            near_scores = lax.dot_general(
                query_feature, near_features, by_row, preferred_element_type=jnp.float32
            )
            top = jnp.max(scores, axis=1, keepdims=True)
            expo = jnp.exp((scores - top) * softmax_scale)
            expo_sum = jnp.sum(expo, axis=1, keepdims=True)
            both = jnp.concatenate(
                [expo.astype(jnp.bfloat16), near_scores.astype(jnp.bfloat16)], axis=0
            )
            summed = jnp.dot(both, near_values, preferred_element_type=jnp.float32)
            near_total = totals[pl.ds(near[0], 1), :]
            for i in near[1:]:
                near_total = near_total + totals[pl.ds(i, 1), :]
            denominator = jnp.sum(
                query_feature.astype(jnp.float32) * (total - near_total), axis=1, keepdims=True
            )
            numerator = (
                jnp.dot(query_feature, high, preferred_element_type=jnp.float32)
                + (
                    jnp.dot(query_feature, middle, preferred_element_type=jnp.float32)
                    + jnp.dot(query_feature, low, preferred_element_type=jnp.float32)
                )
                - summed[BLOCK:]
            )
            linear = (numerator / denominator).astype(jnp.bfloat16)
            out = summed[:BLOCK] / expo_sum + jnp.dot(
                linear, weight_ref[...], preferred_element_type=jnp.float32
            )
            out_refs[part][0, span, :] = out.astype(jnp.bfloat16)


def attend_heads(lists, sent, own_column, other_column, branch_weight, softmax_scale):
    parts = len(sent)
    heads, _, rows, width = sent[0].shape
    blocks = 2 * parts * (rows // BLOCK)
    keys_seen = heads * parts * rows * lists.shape[2] * BLOCK
    query_spec = pl.BlockSpec((1, 1, rows, width), lambda head, _: (head, 0, 0, 0))
    column_spec = pl.BlockSpec((parts, 1, 2, rows, width), lambda head, _: (0, head, 0, 0, 0))
    return pl.pallas_call(
        functools.partial(attend_kernel, softmax_scale, parts),
        grid_spec=pltpu.PrefetchScalarGridSpec(
            num_scalar_prefetch=1,
            grid=(heads,),
            in_specs=[query_spec] * parts
            + [column_spec, column_spec, pl.BlockSpec((width, width), lambda head, _: (0, 0))],
            out_specs=[pl.BlockSpec((1, rows, width), lambda head, _: (head, 0, 0))] * parts,
            scratch_shapes=[pltpu.VMEM((blocks, BLOCK, width), jnp.bfloat16)] * 3
            + [pltpu.VMEM((blocks, width), jnp.float32)],
        ),
        out_shape=[jax.ShapeDtypeStruct((heads, rows, width), jnp.bfloat16)] * parts,
        cost_estimate=pl.CostEstimate(
            flops=heads * 11_000_000_000,
            transcendentals=keys_seen,
            bytes_accessed=heads * 8 * parts * rows * width * 2,
        ),
        compiler_params=pltpu.CompilerParams(vmem_limit_bytes=40 << 20),
        name="attend",
    )(lists, *sent, own_column, other_column, branch_weight)


def as_sent(array):

    def short(part):
        return part.astype(jnp.bfloat16) if part.dtype == jnp.float32 else part

    return jax.tree.map(short, array)


def feature(values_in):
    return jax.nn.elu(values_in) + 1.0


def attend_pair(inputs, pool_keys, pool_values, branch_weight, softmax_scale):
    query_block_rows, query_feature, pool_index, pair_state, pair_total = inputs
    block_count = query_block_rows.shape[0]
    head_width = query_block_rows.shape[-1]
    nearby_key_rows = jnp.take(pool_keys, pool_index.reshape(-1), axis=0).reshape(
        block_count, 2, -1, head_width
    )
    nearby_value_rows = jnp.take(pool_values, pool_index.reshape(-1), axis=0).reshape(
        block_count, 2, -1, head_width
    )
    score_matrix = (
        jnp.einsum(
            "bhqd,bhkd->bhqk", query_block_rows, nearby_key_rows, preferred_element_type=jnp.float32
        )
        * softmax_scale
    )
    top_score = jnp.max(score_matrix, axis=-1, keepdims=True)
    expo_scores = jnp.exp(score_matrix - top_score)
    softmax_weights = (expo_scores / jnp.sum(expo_scores, axis=-1, keepdims=True)).astype(
        jnp.bfloat16
    )
    sparse_output = jnp.einsum(
        "bhqk,bhkd->bhqd", softmax_weights, nearby_value_rows, preferred_element_type=jnp.float32
    )
    nearby_key_features = feature(nearby_key_rows.astype(jnp.float32)).astype(jnp.bfloat16)
    nearby_score_matrix = jnp.einsum(
        "bhqd,bhkd->bhqk", query_feature, nearby_key_features, preferred_element_type=jnp.float32
    )
    nearby_weight_matrix = nearby_score_matrix.astype(jnp.bfloat16)
    nearby_numerator = jnp.einsum(
        "bhqk,bhkd->bhqd",
        nearby_weight_matrix,
        nearby_value_rows,
        preferred_element_type=jnp.float32,
    )
    nearby_denominator = jnp.sum(nearby_score_matrix, axis=-1)
    feature_wide = query_feature.astype(jnp.float32)
    linear_numerator = (
        jnp.einsum("bhqd,hde->bhqe", feature_wide, pair_state, precision=lax.Precision.HIGHEST)
        - nearby_numerator
    )
    linear_denominator = (
        jnp.einsum("bhqd,hd->bhq", feature_wide, pair_total, precision=lax.Precision.HIGHEST)
        - nearby_denominator
    )
    linear_part = (linear_numerator / linear_denominator[..., None]).astype(jnp.bfloat16)
    projected = jnp.einsum(
        "bhqd,de->bhqe", linear_part, branch_weight, preferred_element_type=jnp.float32
    )
    return (sparse_output + projected).astype(jnp.bfloat16)


def exchange_on_device(queries, key_rows, value_rows, critical, branch_weight):
    row_count, head_count, head_width = queries.shape
    list_length = critical.shape[-1]
    block_count = row_count // 64
    shard_count = lax.axis_size(("ctx", "sub"))
    myself = lax.axis_index(("ctx", "sub"))
    local_count = min(block_count, 8)
    pool_size = 24 - local_count
    capacity = (head_count * pool_size + shard_count - 2) // (shard_count - 1)
    softmax_scale = head_width ** (-0.5)
    key_feature = feature(key_rows.astype(jnp.float32)).astype(jnp.bfloat16)
    query_feature = feature(queries.astype(jnp.float32)).astype(jnp.bfloat16)
    kv_state = jnp.einsum(
        "thd,the->hde", key_feature, value_rows, preferred_element_type=jnp.float32
    )
    key_total = jnp.sum(key_feature, axis=0, dtype=jnp.float32)
    kv_state, key_total = lax.psum((kv_state, key_total), ("ctx", "sub"))
    pair_slots = block_count * head_count
    block_owner = critical // block_count
    block_local = critical % block_count
    slot_code = block_local * head_count + jnp.arange(head_count, dtype=jnp.int32)[None, :, None]
    every_block = jnp.arange(shard_count * block_count, dtype=jnp.int32)
    hit_counts = jnp.sum((critical[..., None] == every_block).astype(jnp.int32), axis=(0, 2))
    wanted = (
        hit_counts.reshape(head_count, shard_count, block_count)
        .transpose(1, 2, 0)
        .reshape(shard_count, pair_slots)
        > 0
    )
    wanted = jnp.logical_and(wanted, jnp.arange(shard_count, dtype=jnp.int32)[:, None] != myself)
    slot_place = jnp.cumsum(wanted.astype(jnp.int32), axis=1) - 1
    slot_match = jnp.logical_and(
        wanted[:, :, None],
        slot_place[:, :, None] == jnp.arange(capacity, dtype=jnp.int32)[None, None, :],
    )
    code_values = jnp.sum(
        jnp.where(slot_match, jnp.arange(pair_slots, dtype=jnp.int32)[None, :, None], 0), axis=1
    )
    asked_codes = jnp.where(jnp.any(slot_match, axis=1), code_values, -1)
    local_keys = (
        key_rows.reshape(block_count, 64, head_count, head_width)
        .transpose(0, 2, 1, 3)
        .reshape(pair_slots, 64, head_width)
    )
    local_values = (
        value_rows.reshape(block_count, 64, head_count, head_width)
        .transpose(0, 2, 1, 3)
        .reshape(pair_slots, 64, head_width)
    )
    picked = jnp.clip(
        lax.all_to_all(asked_codes, ("ctx", "sub"), split_axis=0, concat_axis=0, tiled=True),
        0,
        pair_slots - 1,
    )
    far_keys, far_values = lax.all_to_all(
        as_sent((jnp.take(local_keys, picked, axis=0), jnp.take(local_values, picked, axis=0))),
        ("ctx", "sub"),
        split_axis=0,
        concat_axis=0,
        tiled=True,
    )
    pool_keys = jnp.concatenate(
        [local_keys, far_keys.reshape(shard_count * capacity, 64, head_width)], axis=0
    )
    pool_values = jnp.concatenate(
        [local_values, far_values.reshape(shard_count * capacity, 64, head_width)], axis=0
    )
    flat_index = block_owner * pair_slots + slot_code
    slot_table = jnp.where(wanted, slot_place, 0).reshape(-1)
    table_range = jnp.arange(shard_count * pair_slots, dtype=jnp.int32)
    slot_found = jnp.sum(jnp.where(flat_index[..., None] == table_range, slot_table, 0), axis=-1)
    pool_index = jnp.where(
        block_owner == myself, slot_code, pair_slots + block_owner * capacity + slot_found
    )
    pair_count = head_count // 2
    query_pairs = queries.reshape(block_count, 64, pair_count, 2, head_width).transpose(
        2, 0, 3, 1, 4
    )
    feature_pairs = query_feature.reshape(block_count, 64, pair_count, 2, head_width).transpose(
        2, 0, 3, 1, 4
    )
    index_pairs = pool_index.reshape(block_count, pair_count, 2, list_length).transpose(1, 0, 2, 3)
    state_pairs = kv_state.reshape(pair_count, 2, head_width, head_width)
    total_pairs = key_total.reshape(pair_count, 2, head_width)
    attended = lax.map(
        lambda inputs: attend_pair(inputs, pool_keys, pool_values, branch_weight, softmax_scale),
        (query_pairs, feature_pairs, index_pairs, state_pairs, total_pairs),
    )
    return attended.transpose(1, 3, 0, 2, 4).reshape(row_count, head_count, head_width)


def chunk_sizes(heads):
    sizes = [2] * (heads // 2)
    if heads % 2:
        sizes.append(1)
    return sizes


def reshard_on_device(queries, key_rows, value_rows, critical, branch_weight):
    row_count, head_count, head_width = queries.shape
    list_length = critical.shape[-1]
    block_count = row_count // BLOCK
    chips = lax.axis_size("ctx")
    cores = lax.axis_size("sub")
    my_chip = lax.axis_index("ctx")
    my_core = lax.axis_index("sub")
    chip_heads = head_count // chips
    softmax_scale = head_width ** (-0.5)
    swap_cores = [(0, 1), (1, 0)]
    by_head = [array.transpose(1, 0, 2) for array in (queries, key_rows, value_rows)]

    def to_chip(array, distance):
        if distance == 0:
            return array
        return lax.ppermute(array, "ctx", [(chip, chip ^ distance) for chip in range(chips)])

    def heads_of(array, distance, first, size):
        return lax.dynamic_slice_in_dim(
            array, (my_chip ^ distance) * chip_heads + first, size, axis=0
        )

    sent_lists = [
        to_chip(heads_of(critical.transpose(1, 0, 2), distance, 0, chip_heads), distance)
        for distance in range(chips)
    ]
    lists = jnp.stack(sent_lists, axis=1).reshape(chip_heads, chips * block_count, list_length)
    shard = lists // block_count
    lists = (
        (((shard % cores) ^ my_core) * chips + ((shard // cores) ^ my_chip)) * block_count
        + lists % block_count
    )
    attended = jnp.zeros((head_count, row_count, head_width), jnp.bfloat16)
    first = 0
    for size in chunk_sizes(chip_heads):
        sent = []
        for distance in range(chips):
            rows = jnp.stack(
                [heads_of(array, distance, first, size) for array in by_head], axis=1
            )
            sent.append(to_chip(rows, distance))
        own_column = jnp.stack([rows[:, 1:] for rows in sent], axis=0)
        other_column = lax.ppermute(own_column, "sub", swap_cores)
        outs = attend_heads(
            lists[first : first + size],
            sent,
            own_column,
            other_column,
            branch_weight,
            softmax_scale,
        )
        for distance, out in enumerate(outs):
            attended = lax.dynamic_update_slice_in_dim(
                attended,
                to_chip(out, distance),
                (my_chip ^ distance) * chip_heads + first,
                axis=0,
            )
        first += size
    return attended.transpose(1, 0, 2)


def on_device(queries, key_rows, value_rows, critical, branch_weight):
    chips = lax.axis_size("ctx")
    power_of_two = chips & (chips - 1) == 0
    if power_of_two and lax.axis_size("sub") == 2 and queries.shape[1] % chips == 0:
        return reshard_on_device(queries, key_rows, value_rows, critical, branch_weight)
    return exchange_on_device(queries, key_rows, value_rows, critical, branch_weight)


def solution(mesh):
    in_specs = (
        P(("groups", "ctx", "sub"), "head", None),
        P(("groups", "ctx", "sub"), "head", None),
        P(("groups", "ctx", "sub"), "head", None),
        P(("groups", "ctx", "sub"), "head", None),
        P(),
    )
    out_specs = P(("groups", "ctx", "sub"), "head", None)
    return jax.shard_map(
        on_device, mesh=mesh, in_specs=in_specs, out_specs=out_specs, check_vma=False
    )
```
